32 devices in a mesh: row: 4 (over z), col: 8 (over y, x, core).
Axes of the slice: x: 2, y: 2, z: 4, core: 2. Of those that a mesh axis runs over, the one named last changes fastest.
Arguments:
- weight: float32 [16384, 16384], P('row', 'col'), may hold values from -0.046875 to 0.046875
- leak: float32 [16384], P('col'), may hold values from 0.1 to 1
- rates: float32 [3, 256, 16384], P(None, 'row', 'col'), may hold values from -0.95 to 0.95
- cotangent: float32 [256, 16384], P('row', 'col'), may hold values from -2 to 2
Outputs:
- grad_input: float32 [256, 16384], P('row', 'col')
- grad_weight: float32 [16384, 16384], P('row', 'col')
- grad_noise: float32 [3, 16384], P(None, 'row')
The draws below stay inside these ranges and needn't reach their ends.
All inputs are finite; a program needn't handle non-finite values.
Results may differ from the reference program's by a relative error of at most 0.0001.
Values sent between devices are 32-bit elements; how exact they have to be, the bound alone decides.
A program may use at most 192 MiB of HBM per device.

```python
import math
import jax
import jax.numpy as jnp
from jax import lax

N = 16384
B = 256
TSTEPS = 3


def level_of(stream_key, dims, pieces, low, largest):
    level = 1.0
    for axis_at, blocks in pieces:
        heights = jax.random.uniform(jax.random.fold_in(jax.random.fold_in(stream_key, 6), axis_at), (blocks,), jnp.float32, low / len(pieces), largest / len(pieces))
        level = level * jnp.repeat(jnp.exp(heights), dims[axis_at] // blocks).reshape((-1,) + (1,) * (len(dims) - 1 - axis_at))
    return level


def centred(key, shape, deviation, reach, cuts=(), dtype=jnp.bfloat16):
    result = jax.random.normal(key, shape, jnp.float32) * deviation
    if len(cuts) > 0:
        result = level_of(key, shape, cuts, -0.22, 0.18) * result
    return jnp.clip(result, min=-reach, max=reach).astype(dtype)


def setup_inputs(seed: int = 0) -> dict:
    key_of = jax.random.split(jax.random.key(seed), 5)
    weight = centred(key_of[0], (N, N), N ** -0.5, 0.046875, ((0, 4), (1, 8)), jnp.float32)
    leak = jnp.clip(jnp.exp(math.log(1.0) - 2.3025851 * jax.random.uniform(key_of[1], (N,), jnp.float32) ** level_of(key_of[1], (N,), ((0, 8),), -0.2, 0.2)), 0.1, 1.0)
    rates = jnp.clip(jax.random.uniform(key_of[2], (TSTEPS, B, N), jnp.float32, -0.95, 0.95) * level_of(key_of[2], (TSTEPS, B, N), ((1, 4), (2, 8)), -0.4, 0.0), -0.95, 0.95)
    cotangent = centred(key_of[3], (B, N), 0.25, 2.0, ((0, 4), (1, 8)), jnp.float32)
    return {"weight": weight, "leak": leak, "rates": rates, "cotangent": cotangent}


def reference(weight, leak, rates, cotangent):
    carried = cotangent
    grad_weight = jnp.zeros((N, N), jnp.float32)
    noise_list = []
    for step_back in range(TSTEPS - 1, -1, -1):
        scaled = leak[None, :] * carried
        rates_now = rates[step_back]
        noise_list.insert(0, jnp.sum(scaled, axis=0))
        grad_weight = grad_weight + lax.dot_general(scaled, rates_now, (((0,), (0,)), ((), ())), precision=lax.Precision.HIGHEST, preferred_element_type=jnp.float32)
        adjoint = jnp.dot(scaled, weight, precision=lax.Precision.HIGHEST, preferred_element_type=jnp.float32)
        carried = (1.0 - leak[None, :]) * carried + (1.0 - rates_now * rates_now) * adjoint
    return carried, grad_weight, jnp.stack(noise_list)
```

```python
import jax
import jax.numpy as jnp
from jax import lax
from jax.sharding import PartitionSpec as P

TSTEPS = 3
SUBLANES = 8
PREC = lax.Precision.HIGH


def spread_units(scaled, n_row, n_col):
    own_rows, local_units = scaled.shape
    block = own_rows // n_col
    per_row = n_col // n_row
    by_col = lax.all_to_all(
        scaled.reshape(n_col, block, local_units), "col", split_axis=0, concat_axis=0, tiled=True
    )
    by_row = lax.all_to_all(by_col, "row", split_axis=0, concat_axis=0, tiled=True)
    piece = by_row.reshape(n_row, per_row, block, local_units)
    piece = piece.transpose(0, 2, 1, 3).reshape(n_row * block, per_row * local_units)
    return lax.all_gather(piece, "col", axis=0, tiled=True)


def shards_blocks(weight, leak, rates, cotangent):
    n_col = lax.axis_size("col")
    n_row = lax.axis_size("row")
    own_rows, local_units = cotangent.shape
    block = own_rows // n_col
    trials = own_rows * n_row

    def ordered(x):
        y = x.reshape(x.shape[0], n_row, n_col, block, local_units)
        return y.transpose(0, 2, 1, 3, 4).reshape(x.shape[0], trials, local_units)

    full_rates = ordered(lax.all_gather(rates, "row", axis=1, tiled=True))
    noise_list = []
    carried = cotangent
    blocks = []
    for step_back in range(TSTEPS - 1, -1, -1):
        scaled = leak[None, :] * carried
        unit_block = spread_units(scaled, n_row, n_col)
        blocks.append(unit_block)
        noise_list.insert(0, jnp.sum(unit_block, axis=0))
        partial_sum = jnp.dot(unit_block, weight, precision=PREC, preferred_element_type=jnp.float32)
        partial_sum = partial_sum.reshape(n_col, n_row, block, local_units)
        partial_sum = partial_sum.transpose(1, 0, 2, 3).reshape(trials, local_units)
        adjoint = lax.psum_scatter(partial_sum, "row", scatter_dimension=0, tiled=True)
        local_rates = rates[step_back]
        carried = (1.0 - leak[None, :]) * carried + (1.0 - local_rates * local_rates) * adjoint
    dims = (((0,), (0,)), ((), ()))
    early = lax.dot_general(
        jnp.concatenate(blocks[:-1], axis=0),
        jnp.concatenate([full_rates[s] for s in range(TSTEPS - 1, 0, -1)], axis=0),
        dims, precision=PREC, preferred_element_type=jnp.float32,
    )
    grad_weight = early + lax.dot_general(
        blocks[-1], full_rates[0], dims, precision=PREC, preferred_element_type=jnp.float32
    )
    return (carried, grad_weight, jnp.stack(noise_list))


def shards_any(weight, leak, rates, cotangent):
    n_col = lax.axis_size("col")
    own_rows = cotangent.shape[0]
    local_units = cotangent.shape[1]
    full_rates = lax.all_gather(rates, "row", axis=1, tiled=True)
    grad_weight = jnp.zeros(weight.shape, jnp.float32)
    noise_list = []
    carried = cotangent
    for step_back in range(TSTEPS - 1, -1, -1):
        scaled = leak[None, :] * carried
        spread = scaled.reshape(own_rows, local_units // n_col, n_col)
        by_col = lax.all_to_all(spread, "col", split_axis=2, concat_axis=1, tiled=True)
        by_row = lax.all_to_all(by_col, "row", split_axis=1, concat_axis=0, tiled=True)
        gathered = lax.all_gather(by_row, "col", axis=2, tiled=True)
        unit_block = gathered.reshape(gathered.shape[0], gathered.shape[1] * gathered.shape[2])
        rates_now = full_rates[step_back]
        noise_list.insert(0, jnp.sum(unit_block, axis=0))
        grad_weight = grad_weight + lax.dot_general(
            unit_block, rates_now, (((0,), (0,)), ((), ())),
            precision=PREC, preferred_element_type=jnp.float32,
        )
        partial_sum = jnp.dot(unit_block, weight, precision=PREC, preferred_element_type=jnp.float32)
        adjoint = lax.psum_scatter(partial_sum, "row", scatter_dimension=0, tiled=True)
        local_rates = rates[step_back]
        carried = (1.0 - leak[None, :]) * carried + (1.0 - local_rates * local_rates) * adjoint
    return (carried, grad_weight, jnp.stack(noise_list))


def solution(mesh):
    n_row, n_col = mesh.shape["row"], mesh.shape["col"]

    def shards(weight, leak, rates, cotangent):
        fits = cotangent.shape[0] % (n_col * SUBLANES) == 0 and n_col % n_row == 0
        body = shards_blocks if fits else shards_any
        return body(weight, leak, rates, cotangent)

    placed = (P("row", "col"), P("col"), P(None, "row", "col"), P("row", "col"))
    return jax.shard_map(
        shards,
        mesh=mesh,
        in_specs=placed,
        out_specs=(P("row", "col"), P("row", "col"), P(None, "row")),
        check_vma=False,
    )
```

```python
import functools

import jax
import jax.numpy as jnp
from jax import lax
from jax.experimental import pallas as pl
from jax.experimental.pallas import tpu as pltpu
from jax.sharding import PartitionSpec as P

TSTEPS = 3
SUBLANES = 8
CORES = 2
MESH = pl.DeviceIdType.MESH
PREC = lax.Precision.HIGH


def spread_kernel(n_row, n_col, x_ref, out_ref, by_col, by_row, a_send, a_recv, b_send, b_recv,
                  c_send, c_recv, p_send, p_recv, own_sem, f_send, f_recv, keep_sem):
    r, c = lax.axis_index("row"), lax.axis_index("col")
    per_row = n_col // n_row
    n_chip = n_col // CORES
    chip, core = c // CORES, lax.rem(c, CORES)
    partner = chip * CORES + (CORES - 1 - core)

    def remote(src, dst, send, recv, row, col):
        return pltpu.make_async_remote_copy(
            src_ref=src, dst_ref=dst, send_sem=send, recv_sem=recv,
            device_id=(row, col), device_id_type=MESH,
        )

    barrier = pltpu.get_barrier_semaphore()
    for d in range(1, n_col):
        pl.semaphore_signal(barrier, inc=1, device_id=(r, lax.rem(c + d, n_col)), device_id_type=MESH)
    for e in range(1, n_row):
        pl.semaphore_signal(barrier, inc=1, device_id=(lax.rem(r + e, n_row), c), device_id_type=MESH)
    pl.semaphore_wait(barrier, n_col + n_row - 2)

    keep = pltpu.make_async_copy(x_ref.at[c], by_col.at[c], keep_sem)
    keep.start()
    sends = []
    for d in range(1, n_col):
        to = lax.rem(c + d, n_col)
        copy = remote(x_ref.at[to], by_col.at[c], a_send.at[d], a_recv.at[d], r, to)
        copy.start()
        sends.append(copy)
    keep.wait()
    for d in range(1, n_col):
        sends[d - 1].wait_recv()

    def part(k):
        return by_col.at[pl.ds(k * per_row, per_row)]

    for e in range(1, n_row):
        to = lax.rem(r + e, n_row)
        copy = remote(part(to), by_row.at[r], b_send.at[e], b_recv.at[e], to, c)
        copy.start()
        sends.append(copy)

    arrived = []
    local = []
    relays = []

    def relay(e):
        origin = lax.rem(r - e + n_row, n_row)
        for d in range(1, n_chip):
            arrived[e][d - 1].wait_recv()
            source = lax.rem(chip - d + n_chip, n_chip) * CORES + core
            slot = out_ref.at[origin, source]
            copy = remote(slot, slot, f_send.at[e, d], f_recv.at[e, d], r, partner)
            copy.start()
            relays.append(copy)

    for e in range(n_row):
        origin = lax.rem(r - e + n_row, n_row)
        if e == 0:
            piece = part(r)
        else:
            piece = by_row.at[origin]
            remote(part(origin), piece, b_send.at[e], b_recv.at[e], origin, c).wait_recv()
        slot = out_ref.at[origin, c]
        mine = []
        for d in range(1, n_chip):
            to = lax.rem(chip + d, n_chip) * CORES + core
            copy = remote(piece, slot, c_send.at[e, d], c_recv.at[e, d], r, to)
            copy.start()
            mine.append(copy)
        arrived.append(mine)
        copy = remote(piece, slot, p_send.at[e], p_recv.at[e], r, partner)
        copy.start()
        relays.append(copy)
        own = pltpu.make_async_copy(piece, slot, own_sem.at[e])
        own.start()
        local.append(own)
        if e > 0:
            relay(e - 1)
    relay(n_row - 1)
    for copy in sends:
        copy.wait_send()
    for mine in arrived:
        for copy in mine:
            copy.wait_send()
    for copy in relays:
        copy.wait_send()
        copy.wait_recv()
    for own in local:
        own.wait()


def spread_units(scaled, n_row, n_col):
    own_rows, units = scaled.shape
    block = own_rows // n_col
    per_row = n_col // n_row
    n_chip = n_col // CORES
    dma = pltpu.SemaphoreType.DMA
    out = pl.pallas_call(
        functools.partial(spread_kernel, n_row, n_col),
        out_shape=jax.ShapeDtypeStruct((n_row, n_col, per_row, block, units), jnp.float32),
        in_specs=[pl.BlockSpec(memory_space=pltpu.VMEM)],
        out_specs=pl.BlockSpec(memory_space=pl.ANY),
        scratch_shapes=[
            pltpu.VMEM((n_col, block, units), jnp.float32),
            pltpu.VMEM((n_row, per_row, block, units), jnp.float32),
            dma((n_col,)), dma((n_col,)),
            dma((n_row,)), dma((n_row,)),
            dma((n_row, n_chip)), dma((n_row, n_chip)),
            dma((n_row,)), dma((n_row,)), dma((n_row,)),
            dma((n_row, n_chip)), dma((n_row, n_chip)),
            dma,
        ],
        compiler_params=pltpu.CompilerParams(collective_id=0, has_side_effects=True),
        name="spread",
    )(scaled.reshape(n_col, block, units))
    return out.transpose(0, 1, 3, 2, 4).reshape(n_row * own_rows, per_row * units)


def shards_blocks(weight, leak, rates, cotangent):
    n_col = lax.axis_size("col")
    n_row = lax.axis_size("row")
    noise_list = []
    carried = cotangent
    grad_weight = None
    for step_back in range(TSTEPS - 1, -1, -1):
        scaled = leak[None, :] * carried
        scaled, own_rates = lax.optimization_barrier((scaled, rates[step_back]))
        rates_now = lax.all_gather(own_rates, "row", axis=0, tiled=True)
        unit_block = spread_units(scaled, n_row, n_col)
        noise_list.insert(0, jnp.sum(unit_block, axis=0))
        partial_sum = jnp.dot(unit_block, weight, precision=PREC, preferred_element_type=jnp.float32)
        partial_sum, rates_now = lax.optimization_barrier((partial_sum, rates_now))
        adjoint = lax.psum_scatter(partial_sum, "row", scatter_dimension=0, tiled=True)
        product = lax.dot_general(
            unit_block, rates_now, (((0,), (0,)), ((), ())),
            precision=PREC, preferred_element_type=jnp.float32,
        )
        grad_weight = product if grad_weight is None else grad_weight + product
        if step_back > 0:
            adjoint, grad_weight = lax.optimization_barrier((adjoint, grad_weight))
        carried = (1.0 - leak[None, :]) * carried + (1.0 - own_rates * own_rates) * adjoint
    return (carried, grad_weight, jnp.stack(noise_list))


def shards_any(weight, leak, rates, cotangent):
    n_col = lax.axis_size("col")
    own_rows = cotangent.shape[0]
    local_units = cotangent.shape[1]
    full_rates = lax.all_gather(rates, "row", axis=1, tiled=True)
    grad_weight = jnp.zeros(weight.shape, jnp.float32)
    noise_list = []
    carried = cotangent
    for step_back in range(TSTEPS - 1, -1, -1):
        scaled = leak[None, :] * carried
        spread = scaled.reshape(own_rows, local_units // n_col, n_col)
        by_col = lax.all_to_all(spread, "col", split_axis=2, concat_axis=1, tiled=True)
        by_row = lax.all_to_all(by_col, "row", split_axis=1, concat_axis=0, tiled=True)
        gathered = lax.all_gather(by_row, "col", axis=2, tiled=True)
        unit_block = gathered.reshape(gathered.shape[0], gathered.shape[1] * gathered.shape[2])
        rates_now = full_rates[step_back]
        noise_list.insert(0, jnp.sum(unit_block, axis=0))
        grad_weight = grad_weight + lax.dot_general(
            unit_block, rates_now, (((0,), (0,)), ((), ())),
            precision=PREC, preferred_element_type=jnp.float32,
        )
        partial_sum = jnp.dot(unit_block, weight, precision=PREC, preferred_element_type=jnp.float32)
        adjoint = lax.psum_scatter(partial_sum, "row", scatter_dimension=0, tiled=True)
        local_rates = rates[step_back]
        carried = (1.0 - leak[None, :]) * carried + (1.0 - local_rates * local_rates) * adjoint
    return (carried, grad_weight, jnp.stack(noise_list))


def solution(mesh):
    n_row, n_col = mesh.shape["row"], mesh.shape["col"]

    def shards(weight, leak, rates, cotangent):
        fits = cotangent.shape[0] % (n_col * SUBLANES) == 0 and n_col % n_row == 0 and n_col % CORES == 0
        body = shards_blocks if fits else shards_any
        return body(weight, leak, rates, cotangent)

    placed = (P("row", "col"), P("col"), P(None, "row", "col"), P("row", "col"))
    return jax.shard_map(
        shards,
        mesh=mesh,
        in_specs=placed,
        out_specs=(P("row", "col"), P("row", "col"), P(None, "row")),
        check_vma=False,
    )
```

```python
import functools

import jax
import jax.numpy as jnp
from jax import lax
from jax.experimental import pallas as pl
from jax.experimental.pallas import tpu as pltpu
from jax.sharding import PartitionSpec as P

TSTEPS = 3
SUBLANES = 8
CORES = 2
SPLIT = 4
MESH = pl.DeviceIdType.MESH
PREC = lax.Precision.HIGH


def spread_kernel(n_row, n_col, x_ref, out_ref, by_col, by_row, a_send, a_recv, b_send, b_recv,
                  c_send, c_recv, p_send, p_recv, own_sem, f_send, f_recv, keep_sem):
    r, c = lax.axis_index("row"), lax.axis_index("col")
    per_row = n_col // n_row
    n_chip = n_col // CORES
    chip, core = c // CORES, lax.rem(c, CORES)
    partner = chip * CORES + (CORES - 1 - core)

    def remote(src, dst, send, recv, row, col):
        return pltpu.make_async_remote_copy(
            src_ref=src, dst_ref=dst, send_sem=send, recv_sem=recv,
            device_id=(row, col), device_id_type=MESH,
        )

    barrier = pltpu.get_barrier_semaphore()
    for d in range(1, n_col):
        pl.semaphore_signal(barrier, inc=1, device_id=(r, lax.rem(c + d, n_col)), device_id_type=MESH)
    for e in range(1, n_row):
        pl.semaphore_signal(barrier, inc=1, device_id=(lax.rem(r + e, n_row), c), device_id_type=MESH)
    pl.semaphore_wait(barrier, n_col + n_row - 2)

    keep = pltpu.make_async_copy(x_ref.at[c], by_col.at[c], keep_sem)
    keep.start()
    sends = []
    for d in range(1, n_col):
        to = lax.rem(c + d, n_col)
        copy = remote(x_ref.at[to], by_col.at[c], a_send.at[d], a_recv.at[d], r, to)
        copy.start()
        sends.append(copy)
    keep.wait()
    for d in range(1, n_col):
        sends[d - 1].wait_recv()

    def part(k):
        return by_col.at[pl.ds(k * per_row, per_row)]

    for e in range(1, n_row):
        to = lax.rem(r + e, n_row)
        copy = remote(part(to), by_row.at[r], b_send.at[e], b_recv.at[e], to, c)
        copy.start()
        sends.append(copy)

    arrived = []
    local = []
    relays = []

    def relay(e):
        origin = lax.rem(r - e + n_row, n_row)
        for d in range(1, n_chip):
            arrived[e][d - 1].wait_recv()
            source = lax.rem(chip - d + n_chip, n_chip) * CORES + core
            slot = out_ref.at[origin, source]
            copy = remote(slot, slot, f_send.at[e, d], f_recv.at[e, d], r, partner)
            copy.start()
            relays.append(copy)

    for e in range(n_row):
        origin = lax.rem(r - e + n_row, n_row)
        if e == 0:
            piece = part(r)
        else:
            piece = by_row.at[origin]
            remote(part(origin), piece, b_send.at[e], b_recv.at[e], origin, c).wait_recv()
        slot = out_ref.at[origin, c]
        mine = []
        for d in range(1, n_chip):
            to = lax.rem(chip + d, n_chip) * CORES + core
            copy = remote(piece, slot, c_send.at[e, d], c_recv.at[e, d], r, to)
            copy.start()
            mine.append(copy)
        arrived.append(mine)
        copy = remote(piece, slot, p_send.at[e], p_recv.at[e], r, partner)
        copy.start()
        relays.append(copy)
        own = pltpu.make_async_copy(piece, slot, own_sem.at[e])
        own.start()
        local.append(own)
        if e > 0:
            relay(e - 1)
    relay(n_row - 1)
    for copy in sends:
        copy.wait_send()
    for mine in arrived:
        for copy in mine:
            copy.wait_send()
    for copy in relays:
        copy.wait_send()
        copy.wait_recv()
    for own in local:
        own.wait()


def spread_units(scaled, n_row, n_col):
    own_rows, units = scaled.shape
    block = own_rows // n_col
    per_row = n_col // n_row
    n_chip = n_col // CORES
    dma = pltpu.SemaphoreType.DMA
    out = pl.pallas_call(
        functools.partial(spread_kernel, n_row, n_col),
        out_shape=jax.ShapeDtypeStruct((n_row, n_col, per_row, block, units), jnp.float32),
        in_specs=[pl.BlockSpec(memory_space=pltpu.VMEM)],
        out_specs=pl.BlockSpec(memory_space=pl.ANY),
        scratch_shapes=[
            pltpu.VMEM((n_col, block, units), jnp.float32),
            pltpu.VMEM((n_row, per_row, block, units), jnp.float32),
            dma((n_col,)), dma((n_col,)),
            dma((n_row,)), dma((n_row,)),
            dma((n_row, n_chip)), dma((n_row, n_chip)),
            dma((n_row,)), dma((n_row,)), dma((n_row,)),
            dma((n_row, n_chip)), dma((n_row, n_chip)),
            dma,
        ],
        compiler_params=pltpu.CompilerParams(collective_id=0, has_side_effects=True),
        name="spread",
    )(scaled.reshape(n_col, block, units))
    return out.transpose(0, 1, 3, 2, 4).reshape(n_row * own_rows, per_row * units)


def shards_blocks(weight, leak, rates, cotangent):
    n_col = lax.axis_size("col")
    n_row = lax.axis_size("row")
    noise_list = []
    carried = cotangent
    grad_weight = None
    for step_back in range(TSTEPS - 1, -1, -1):
        scaled = leak[None, :] * carried
        scaled, own_rates = lax.optimization_barrier((scaled, rates[step_back]))
        rates_now = lax.all_gather(own_rates, "row", axis=0, tiled=True)
        unit_block = spread_units(scaled, n_row, n_col)
        units = weight.shape[1]
        first = units // SPLIT
        head = jnp.dot(unit_block, weight[:, :first], precision=PREC, preferred_element_type=jnp.float32)
        head, unit_block = lax.optimization_barrier((head, unit_block))
        head_sum = lax.psum_scatter(head, "row", scatter_dimension=0, tiled=True)
        tail = jnp.dot(unit_block, weight[:, first:], precision=PREC, preferred_element_type=jnp.float32)
        tail, rates_now, unit_block = lax.optimization_barrier((tail, rates_now, unit_block))
        tail_sum = lax.psum_scatter(tail, "row", scatter_dimension=0, tiled=True)
        product = lax.dot_general(
            unit_block, rates_now, (((0,), (0,)), ((), ())),
            precision=PREC, preferred_element_type=jnp.float32,
        )
        grad_weight = product if grad_weight is None else grad_weight + product
        noise = jnp.sum(unit_block, axis=0)
        if step_back > 0:
            head_sum, tail_sum, grad_weight, noise = lax.optimization_barrier(
                (head_sum, tail_sum, grad_weight, noise)
            )
        noise_list.insert(0, noise)
        adjoint = jnp.concatenate([head_sum, tail_sum], axis=1)
        carried = (1.0 - leak[None, :]) * carried + (1.0 - own_rates * own_rates) * adjoint
    return (carried, grad_weight, jnp.stack(noise_list))


def shards_any(weight, leak, rates, cotangent):
    n_col = lax.axis_size("col")
    own_rows = cotangent.shape[0]
    local_units = cotangent.shape[1]
    full_rates = lax.all_gather(rates, "row", axis=1, tiled=True)
    grad_weight = jnp.zeros(weight.shape, jnp.float32)
    noise_list = []
    carried = cotangent
    for step_back in range(TSTEPS - 1, -1, -1):
        scaled = leak[None, :] * carried
        spread = scaled.reshape(own_rows, local_units // n_col, n_col)
        by_col = lax.all_to_all(spread, "col", split_axis=2, concat_axis=1, tiled=True)
        by_row = lax.all_to_all(by_col, "row", split_axis=1, concat_axis=0, tiled=True)
        gathered = lax.all_gather(by_row, "col", axis=2, tiled=True)
        unit_block = gathered.reshape(gathered.shape[0], gathered.shape[1] * gathered.shape[2])
        rates_now = full_rates[step_back]
        noise_list.insert(0, jnp.sum(unit_block, axis=0))
        grad_weight = grad_weight + lax.dot_general(
            unit_block, rates_now, (((0,), (0,)), ((), ())),
            precision=PREC, preferred_element_type=jnp.float32,
        )
        partial_sum = jnp.dot(unit_block, weight, precision=PREC, preferred_element_type=jnp.float32)
        adjoint = lax.psum_scatter(partial_sum, "row", scatter_dimension=0, tiled=True)
        local_rates = rates[step_back]
        carried = (1.0 - leak[None, :]) * carried + (1.0 - local_rates * local_rates) * adjoint
    return (carried, grad_weight, jnp.stack(noise_list))


def solution(mesh):
    n_row, n_col = mesh.shape["row"], mesh.shape["col"]

    def shards(weight, leak, rates, cotangent):
        fits = cotangent.shape[0] % (n_col * SUBLANES) == 0 and n_col % n_row == 0 and n_col % CORES == 0
        body = shards_blocks if fits else shards_any
        return body(weight, leak, rates, cotangent)

    placed = (P("row", "col"), P("col"), P(None, "row", "col"), P("row", "col"))
    return jax.shard_map(
        shards,
        mesh=mesh,
        in_specs=placed,
        out_specs=(P("row", "col"), P("row", "col"), P(None, "row")),
        check_vma=False,
    )
```
